32 devices in a mesh: groups: 2 (over y), pairs: 4 (over z), section: 2 (over core), sub: 2 (over x).
Axes of the slice: x: 2, y: 2, z: 4, core: 2. Of those that a mesh axis runs over, the one named last changes fastest.
Arguments:
- raw_record: bfloat16 [64, 49152], P(('groups', 'pairs', 'section'), 'sub'), parts along dimension 0, may hold values from -6 to 6
- fir_taps: float32 [64], replicated, may hold values from -0.75 to 0.75
- channel_ids: int32 [64], P('groups'), parts along dimension 0, may hold values from 0 to 31, each once
- offsets: int32 [8], P(('groups', 'sub')), parts along dimension 0, may hold values from 0 to 16324
- pair_table: int32 [32, 2], P('groups'), parts along dimension 0, may hold values from -1 to 3, as said below
Outputs:
- correlations: float32 [8, 32, 8, 2048], P(('section', 'sub'), ('groups', 'pairs')), parts along dimension 1
The draws below stay inside these ranges and needn't reach their ends.
There are 2 independent parts, one for each index of `groups`. The reference program is written for one: setup_inputs(seed, part) draws one part's arguments, and reference() takes and returns one part's arrays. A program takes and returns all parts, laid end to end along the dimension named above; an argument that names none is the same for every part. Nothing has to cross between parts.
Inputs may be any that keep to these rules, and one draw needn't show every extreme that they name: `pair_table`: each row is a pair block (I, J) with I <= J, or (-1, -1) for an empty slot. Every pair block of the 4 x 4 triangle stands in exactly one slot; all live slots of one owner share the first block I; owners p and p + 2 together hold exactly 5 pair blocks; some owner fills all 4 slots.
All inputs are finite; a program needn't handle non-finite values.
Results may differ from the reference program's by a relative error of at most 0.0075.
Values may be sent and summed in bfloat16 or wider, within the bound.
A program may use at most 128 MiB of HBM per device.

```python
import math
import jax
import jax.numpy as jnp
from jax import lax

NF = 2048
TAPS = 64
DEC = 4
BAND = 64
NSUB_DEV = 2
SPAN = 24576
NSUB = 4
CH = 32
BLK = 8
CB = 4
SLOTS = 4
N_PAIRS = 4
N_SUB = 2


def draw_pair_table(key, part):
    half_pairs = N_PAIRS // 2
    key_rows, key_flip, key_slots = jax.random.split(key, 3)
    row_pairs = jax.random.permutation(key_rows, half_pairs).astype(jnp.int32)
    flipped = jax.random.randint(key_flip, (half_pairs,), 0, 2).astype(jnp.int32)
    chip_index = jnp.arange(N_PAIRS, dtype=jnp.int32)
    column = chip_index % half_pairs
    low_row = row_pairs[column]
    is_upper = chip_index // half_pairs
    block_row = jnp.where(is_upper == flipped[column], low_row, CB - 1 - low_row)
    scores = jax.random.randint(key_slots, (N_PAIRS, SLOTS), 0, 1 << 20).astype(jnp.int32) * SLOTS + jnp.arange(SLOTS, dtype=jnp.int32)[None, :]
    entry_at_slot = jnp.argsort(scores, axis=1).astype(jnp.int32)
    live_count = CB - block_row
    live_entry = entry_at_slot < live_count[:, None]
    first_block = jnp.where(live_entry, block_row[:, None], -1)
    second_block = jnp.where(live_entry, block_row[:, None] + entry_at_slot, -1)
    return jnp.stack([first_block, second_block], axis=-1).reshape(N_PAIRS * SLOTS, 2).astype(jnp.int32)


def place_ends(values, stream_key, low, top_value):
    shape = values.shape
    place = [jax.random.randint(jax.random.fold_in(stream_key, axis), (), 0, shape[axis]) for axis in range(len(shape))]
    values = values.at[tuple(place)].set(low)
    longest = shape.index(max(shape))
    place[longest] = (place[longest] + 1) % shape[longest]
    return values.at[tuple(place)].set(top_value)


def block_levels(stream_key, shape, pieces, least, top_value):
    factor_of = 1.0
    for dim, blocks in pieces:
        steps = jax.random.uniform(jax.random.fold_in(jax.random.fold_in(stream_key, 6), dim), (blocks,), jnp.float32, least / len(pieces), top_value / len(pieces))
        factor_of = factor_of * jnp.repeat(jnp.exp(steps), shape[dim] // blocks).reshape((-1,) + (1,) * (len(shape) - 1 - dim))
    return factor_of


def centred(key, shape, deviation, reach, pieces=(), kind=jnp.bfloat16):
    level = block_levels(key, shape, pieces, -0.22, 0.18) if pieces else 1.0
    entries = jax.random.normal(key, shape, jnp.float32) * deviation * level
    return jnp.minimum(jnp.maximum(entries, -reach), reach).astype(kind)


def setup_inputs(seed: int = 0, part: int = 0) -> dict:
    arg_keys = jax.random.split(jax.random.key(seed), 6)
    part_keys = jax.random.split(jax.random.fold_in(arg_keys[5], part), 6)
    raw_record = centred(part_keys[0], (CH, N_SUB * SPAN), 1.0, 6.0, ((0, 8), (1, 2)))
    fir_taps = centred(arg_keys[1], (TAPS,), TAPS ** -0.5, 0.75, (), jnp.float32)
    channel_ids = jax.random.permutation(part_keys[2], CH).astype(jnp.int32)
    offsets = place_ends(jax.random.randint(part_keys[3], (NSUB,), 0, SPAN - DEC * (NF - 1) - TAPS + 1), jax.random.fold_in(part_keys[3], 1), 0, SPAN - DEC * (NF - 1) - TAPS).astype(jnp.int32)
    pair_table = draw_pair_table(jax.random.fold_in(jax.random.fold_in(arg_keys[5], part), 71), part)
    return {"raw_record": raw_record, "fir_taps": fir_taps, "channel_ids": channel_ids, "offsets": offsets, "pair_table": pair_table}


def forward_table(length):
    sample = jnp.arange(length, dtype=jnp.int32)[:, None]
    bin_index = jnp.arange(length // 2, dtype=jnp.int32)[None, :]
    angles = (sample * bin_index % length).astype(jnp.float32) * (2.0 * math.pi / length)
    return jnp.concatenate([jnp.cos(angles), -jnp.sin(angles)], axis=1).astype(jnp.bfloat16)

def inverse_table(length):
    bin_index = jnp.arange(length // 2, dtype=jnp.int32)[:, None]
    lag_index = jnp.arange(length, dtype=jnp.int32)[None, :]
    shifted = (lag_index + length // 2) % length
    angles = (bin_index * shifted % length).astype(jnp.float32) * (2.0 * math.pi / length)
    weight = jnp.where(bin_index == 0, 1.0, 2.0).astype(jnp.float32) / math.sqrt(length)
    return jnp.concatenate([weight * jnp.cos(angles), -weight * jnp.sin(angles)], axis=0).astype(jnp.bfloat16)

def whiten(spectrum):
    power_all = spectrum[:, :, 0] ** 2 + spectrum[:, :, 1] ** 2
    extent = power_all.shape
    banded = lax.optimization_barrier(jnp.mean(power_all.reshape(extent[0], extent[1], extent[2] // BAND, BAND), axis=-1))
    inverse_rms = jnp.repeat(lax.rsqrt(banded + 1e-06), BAND, axis=-1)
    return (spectrum * inverse_rms[:, :, None, :]).astype(jnp.bfloat16)

def reference(raw_record, fir_taps, channel_ids, offsets, pair_table):
    seg_len = DEC * (NF - 1) + TAPS
    starts = jnp.arange(NSUB, dtype=jnp.int32) // NSUB_DEV * SPAN + offsets

    def cut_window(start_at):
        return lax.dynamic_slice_in_dim(raw_record, start_at, seg_len, 1)
    windows = jax.vmap(cut_window, out_axes=1)(starts).astype(jnp.float32)
    accum = jnp.zeros((CH, NSUB, NF), jnp.float32)
    for tap_index in range(TAPS):
        accum = accum + fir_taps[tap_index] * windows[:, :, tap_index:tap_index + DEC * (NF - 1) + 1:DEC]
    decimated = accum.astype(jnp.bfloat16)
    spectrum = jnp.dot(decimated.reshape(CH * NSUB, NF), forward_table(NF), preferred_element_type=jnp.float32)
    whitened = whiten(spectrum.reshape(CH, NSUB, 2, NF // 2))
    by_channel = jnp.take(whitened, jnp.argsort(channel_ids).astype(jnp.int32), axis=0)
    lag_table = inverse_table(NF)

    def one_slot(slot_entry):
        live_slot = slot_entry[0] >= 0
        first_rows = lax.dynamic_slice_in_dim(by_channel, jnp.maximum(slot_entry[0], 0) * BLK, BLK, 0).astype(jnp.float32)
        second_rows = lax.dynamic_slice_in_dim(by_channel, jnp.maximum(slot_entry[1], 0) * BLK, BLK, 0).astype(jnp.float32)
        real_part = jnp.einsum('awk,bwk->abk', first_rows[:, :, 0], second_rows[:, :, 0]) + jnp.einsum('awk,bwk->abk', first_rows[:, :, 1], second_rows[:, :, 1])
        imag_part = jnp.einsum('awk,bwk->abk', first_rows[:, :, 1], second_rows[:, :, 0]) - jnp.einsum('awk,bwk->abk', first_rows[:, :, 0], second_rows[:, :, 1])
        cross_bins = jnp.stack([real_part, imag_part], axis=2) / NSUB
        cross_bins = jnp.where(live_slot, cross_bins, 0.0).astype(jnp.bfloat16)
        return jnp.dot(cross_bins.reshape(BLK * BLK, NF), lag_table, preferred_element_type=jnp.float32).reshape(BLK, BLK, NF)
    all_lags = lax.map(one_slot, pair_table)
    return jnp.transpose(all_lags, (1, 0, 2, 3))
```

```python
import functools
import math

import jax
import jax.numpy as jnp
import numpy as np
from jax import lax
from jax.experimental import pallas as pl
from jax.experimental.pallas import tpu as pltpu
from jax.sharding import PartitionSpec as P

NF = 2048
TAPS = 64
DEC = 4
BAND = 64
LANES = 128
RADIX = 8
HALF = 4
FINE = LANES // DEC
REACH = 3
SPREAD = REACH + DEC - 1
PIECES = DEC * (NF // LANES)
MESH = pl.DeviceIdType.MESH


def round_bf16(values):
    return np.asarray(values).astype(jnp.bfloat16)


@functools.cache
def tables():
    kappa = np.arange(LANES)
    angle = 2 * np.pi * (kappa[:, None] * kappa[None, :] % (2 * LANES)) / (2 * LANES)
    c, s = np.cos(angle), np.sin(angle)
    dft = np.block([[c, -s], [s, c]])
    high = round_bf16(dft)
    low = round_bf16(dft - high.astype(np.float64))
    forward = np.concatenate([high, low], axis=0)
    n1 = (np.arange(8) // HALF * LANES)[:, None] + kappa[None, :]
    turn = 2 * np.pi * np.arange(RADIX)[:, None, None] * n1[None] / NF
    twiddle = np.stack([np.cos(turn), np.sin(turn)], axis=1).astype(np.float32)
    weight = 2.0 / math.sqrt(NF)
    cols = []
    for h in range(2):
        j1 = h * LANES + kappa
        theta = 2 * np.pi * (kappa[:, None] * j1[None, :] % (2 * LANES)) / (2 * LANES)
        c, s = weight * np.cos(theta), weight * np.sin(theta)
        cols.append(np.block([[c, s], [-s, c]]))
    inverse = round_bf16(np.concatenate(cols, axis=1))
    turn = 2 * np.pi * np.arange(RADIX)[:, None] * np.arange(2 * LANES)[None, :] / NF
    back = np.concatenate([np.cos(turn), np.sin(turn)], axis=0).astype(np.float32)
    return forward, twiddle, inverse, back


def spread8(d):
    c = math.sqrt(0.5)
    a = [d[i] + d[i + 4] for i in range(4)]
    m = [d[i] - d[i + 4] for i in range(4)]
    even, odd = a[0] + a[2], a[1] + a[3]
    u, v = c * (m[1] - m[3]), c * (m[1] + m[3])
    y1 = (m[0] + u, -m[2] - v)
    y3 = (m[0] - u, m[2] - v)
    y2 = (a[0] - a[2], a[3] - a[1])
    back = [(r, -i) for r, i in (y3, y2, y1)]
    return [(even + odd, None), y1, y2, y3, (even - odd, None)] + back


def gather8(x):
    c = math.sqrt(0.5)
    e0, o0 = x[0][0] + x[4][0], x[0][0] - x[4][0]
    p = [x[b][0] + x[8 - b][0] for b in (1, 2, 3)]
    q = [x[8 - b][1] - x[b][1] for b in (1, 2, 3)]
    pp, pm = p[0] + p[2], c * (p[0] - p[2])
    qm, qp = q[0] - q[2], c * (q[0] + q[2])
    ep, em = e0 + p[1], e0 - p[1]
    op, om = o0 + q[1], o0 - q[1]
    f, g = pm + qp, pm - qp
    return [ep + pp, op + f, em + qm, om - g, ep - pp, op - f, em - qm, om + g]


def kernel(sizes, raw_in, taps_in, ids_in, offs_in, table_in, forward_in, twiddle_in, inverse_in, back_in, out,
           raw, taps, ids, offs, table, forward, twiddle, in_sems,
           held, tapf, shifted, lhs, inv, back, late_sems, z_send, x_send, c_send, recv):
    pairs, subs, rows, wins, slots, leads = sizes
    unit = rows * wins
    block = 2 * rows
    p = lax.axis_index("pairs")
    sec = lax.axis_index("section")
    sub = lax.axis_index("sub")

    barrier = pltpu.get_barrier_semaphore()
    for dp in range(pairs):
        for d in range(subs):
            if dp or d:
                pl.semaphore_signal(
                    barrier, inc=1, device_id_type=MESH,
                    device_id={"pairs": lax.rem(p + dp, pairs), "sub": lax.rem(sub + d, subs)})
    pl.semaphore_signal(barrier, inc=1, device_id={"section": 1 - sec}, device_id_type=MESH)

    loads = [
        pltpu.make_async_copy(source, target, in_sems.at[i])
        for i, (source, target) in enumerate(
            ((taps_in, taps), (offs_in, offs), (raw_in, raw.at[:, pl.ds(0, raw_in.shape[1])]), (forward_in, forward),
             (twiddle_in, twiddle), (ids_in, ids), (table_in, table)))
    ]
    for load in loads:
        load.start()
    late = [
        pltpu.make_async_copy(source, target, late_sems.at[i])
        for i, (source, target) in enumerate(((inverse_in, inv), (back_in, back)))
    ]
    for load in late:
        load.start()
    tapf[...] = jnp.zeros_like(tapf)
    span = raw_in.shape[1]
    raw[:, span:] = jnp.zeros((rows, raw.shape[1] - span), raw.dtype)
    seg = lax.broadcasted_iota(jnp.int32, (2 * LANES, LANES), 0) % LANES // RADIX
    same = seg == lax.broadcasted_iota(jnp.int32, (2 * LANES, LANES), 1) // RADIX
    mean = jnp.where(same, 1.0 / BAND, 0.0).astype(jnp.bfloat16)
    sign = 1.0 - 2.0 * (lax.broadcasted_iota(jnp.int32, (8, LANES), 1) % 2).astype(jnp.float32)
    line8 = lax.broadcasted_iota(jnp.int32, (8, LANES), 0)
    top = line8 < HALF
    lane = lax.broadcasted_iota(jnp.int32, (FINE, LANES), 1)
    step = DEC * lax.broadcasted_iota(jnp.int32, (FINE, LANES), 0)
    for load in loads:
        load.wait()
    tapf[0:1, 0:TAPS] = taps[...]
    moved = jnp.broadcast_to(tapf[0:1, :], (8, LANES))
    for b in range(3):
        moved = jnp.where((line8 >> b) & 1 == 1, pltpu.roll(moved, 1 << b, 1), moved)
    for i in range(LANES // 8):
        ahead = pltpu.roll(moved, 8 * i, 1) if i else moved
        shifted[8 * i : 8 * i + 8, :] = ahead
        shifted[LANES + 8 * i : LANES + 8 * i + 8, :] = ahead
    blank = jnp.zeros((FINE, LANES), jnp.bfloat16)

    turned = []
    for w in range(wins):
        off = offs[w]
        first, rest = off // LANES, off % LANES
        rolled = shifted[pl.ds(rest, FINE, stride=DEC), :]
        highs, lows = [], []
        for s in range(REACH):
            t = lane + s * LANES - step - rest
            x = jnp.where((t >= 0) & (t < TAPS), rolled, 0.0)
            highs.append(x.astype(jnp.bfloat16))
            lows.append((x - highs[-1].astype(jnp.float32)).astype(jnp.bfloat16))
        cols = []
        for s in range(SPREAD):
            cols.append(jnp.concatenate(
                [part[s - f] if 0 <= s - f < REACH else blank for part in (highs, lows) for f in range(DEC)], axis=0))
        toeplitz = jnp.concatenate(cols, axis=1)
        seen = raw[:, pl.ds(first * LANES, (PIECES + SPREAD - DEC) * LANES)].astype(jnp.float32)
        piece = [seen[:, m * LANES : (m + 1) * LANES] for m in range(PIECES + SPREAD - DEC)]
        pair = [jnp.concatenate([piece[m], piece[m + DEC]], axis=0) for m in range(len(piece) - DEC)]
        data = jnp.concatenate(
            [jnp.concatenate([pair[s + 2 * DEC * n] for n in range(RADIX)], axis=0).astype(jnp.bfloat16)
             for s in range(SPREAD)], axis=1)
        total = lax.dot_general(data, toeplitz, (((1,), (1,)), ((), ())), preferred_element_type=jnp.float32)
        deci = (total[:, :LANES] + total[:, LANES:]).astype(jnp.bfloat16).astype(jnp.float32)
        parts = spread8([deci[8 * n : 8 * n + 8] for n in range(RADIX)])
        for b in range(RADIX):
            re, im = parts[b]
            c, s = twiddle[b, 0], twiddle[b, 1]
            if b == 0:
                re, im = re, jnp.zeros_like(re)
            elif im is None:
                re, im = re * c, -re * s
            else:
                re, im = re * c + im * s, im * c - re * s
            turned.append(jnp.concatenate([re, im], axis=1))
    z = jnp.concatenate(turned, axis=0)
    high = z.astype(jnp.bfloat16)
    low = (z - high.astype(jnp.float32)).astype(jnp.bfloat16)
    count_z = z.shape[0]
    both = jnp.dot(jnp.concatenate([high, low], axis=0), forward[: 2 * LANES, :], preferred_element_type=jnp.float32)
    both = both[:count_z] + both[count_z:] + jnp.dot(
        high, forward[2 * LANES :, :], preferred_element_type=jnp.float32)
    spectra = []
    power = None
    for b in range(RADIX):
        for part in range(2):
            lanes = slice(part * LANES, (part + 1) * LANES)
            u0 = both[b * 8 : b * 8 + 8, lanes]
            u1 = both[(RADIX + b) * 8 : (RADIX + b) * 8 + 8, lanes]
            near = jnp.where(top, u0, pltpu.roll(u1, HALF, 0))
            far = jnp.where(top, pltpu.roll(u0, HALF, 0), u1)
            x = near + sign * far
            spectra.append(x)
            power = x * x if power is None else power + x * x
    high = power.astype(jnp.bfloat16)
    low = (power - high.astype(jnp.float32)).astype(jnp.bfloat16)
    band = jnp.dot(jnp.concatenate([high, low], axis=1), mean, preferred_element_type=jnp.float32)
    gain = lax.rsqrt(band + 1e-06)
    mine = (p * 2 + sec) * subs + sub
    for b in range(RADIX):
        held[mine, :, b * LANES : (b + 1) * LANES] = jnp.concatenate(
            [spectra[2 * b] * gain, spectra[2 * b + 1] * gain], axis=0).astype(jnp.bfloat16)

    pl.semaphore_wait(barrier, pairs * subs)

    def send(slot, send_sem, device):
        return pltpu.make_async_remote_copy(
            src_ref=held.at[slot], dst_ref=held.at[slot], send_sem=send_sem,
            recv_sem=recv.at[slot], device_id=device, device_id_type=MESH)

    near = [p]
    for i in range(1, pairs):
        at = jnp.int32(0)
        for q in range(pairs):
            at = jnp.where(p == q, sorted(range(pairs), key=lambda t: (abs(t - q), t))[i], at)
        near.append(at)
    copies = []
    for dp in range(pairs - 1, -1, -1):
        for d in range(subs - 1, -1, -1):
            if not (dp or d):
                continue
            copies.append(send(mine, x_send.at[dp, d], {"pairs": near[dp], "sub": lax.rem(sub + d, subs)}))
            copies[-1].start()
    for dp in range(pairs):
        slot = (near[dp] * 2 + sec) * subs + sub
        if dp:
            send(slot, z_send.at[0], {"section": 1 - sec}).wait_recv()
        copies.append(send(slot, c_send.at[dp, 0], {"section": 1 - sec}))
        copies[-1].start()
    for dp in range(pairs):
        for d in range(1, subs):
            slot = (near[dp] * 2 + sec) * subs + lax.rem(sub + d, subs)
            send(slot, z_send.at[0], {"section": 1 - sec}).wait_recv()
            copies.append(send(slot, c_send.at[dp, d], {"section": 1 - sec}))
            copies[-1].start()

    count = pairs * block
    tall = 2 * unit
    depth = pairs * 2 * subs * tall
    col = lax.broadcasted_iota(jnp.int32, (1, depth), 1)
    col_row = (col // (tall * subs)) * rows + col % rows
    col_id = jnp.full((1, depth), -1, jnp.int32)
    for i in range(count):
        col_id = jnp.where(col_row == i, ids[i], col_id)
    own = table[0, p * slots]
    for s in range(1, slots):
        own = jnp.maximum(own, table[0, p * slots + s])
    group = subs * tall
    line = lax.broadcasted_iota(jnp.int32, (2 * leads * group, 1), 0)
    lead = own * block + (sec * subs + sub) * leads + line // group % leads
    place = line // tall % subs * wins + line // rows % wins
    col_place = col // tall % subs * wins + col // rows % wins
    line_part, col_part = line // unit % 2, col // unit % 2
    crossing = line // (group * leads)
    chosen = (lead == col_id) & (place == col_place) & ((line_part + crossing) % 2 == col_part)
    value = jnp.where((crossing == 1) & (line_part == 1), -1.0, 1.0)
    pick = jnp.where(chosen, value, 0.0).astype(jnp.bfloat16)
    entry = lax.broadcasted_iota(jnp.int32, (slots * block, 1), 0)
    want = jnp.full((slots * block, 1), -1, jnp.int32)
    for s in range(slots):
        live = jnp.where(table[0, p * slots + s] >= 0, table[1, p * slots + s] * block, -block)
        want = jnp.where(entry // block == s, live + entry % block, want)
    order = jnp.where(want == col_id, 1.0 / (wins * subs), 0.0).astype(jnp.bfloat16)

    for dp in range(pairs):
        for d in range(subs):
            slot = (lax.rem(p + dp, pairs) * 2 + 1 - sec) * subs + lax.rem(sub + d, subs)
            send(slot, z_send.at[0], {"section": 1 - sec}).wait_recv()

    width = 2 * LANES
    wanted = slots * block
    edge = jnp.where(lax.broadcasted_iota(jnp.int32, (wanted, LANES), 1) == 0, 0.5, 1.0)
    for base in range(0, RADIX, 2):
        flat = held[:, :, base * LANES : (base + 2) * LANES].reshape(depth, width)
        heads = jnp.dot(pick, flat, preferred_element_type=jnp.float32).astype(jnp.bfloat16)
        for a in range(leads):
            for part in range(2):
                at = (part * leads + a) * group
                full = jnp.concatenate([heads[at : at + group, :]] * (pairs * 2), axis=0)
                got = jnp.dot(order, flat * full, preferred_element_type=jnp.float32)
                for h in range(2):
                    x = got[:, h * LANES : (h + 1) * LANES]
                    if base + h == 0:
                        x = x * edge
                    lhs[base + h, a * wanted : (a + 1) * wanted, part * LANES : (part + 1) * LANES] = x.astype(jnp.bfloat16)

    for load in late:
        load.wait()

    for h in range(2):
        for a in range(leads):
            x = lhs[:, a * wanted : (a + 1) * wanted, :].reshape(RADIX * wanted, width)
            y = jnp.dot(x, inv[:, h * width : (h + 1) * width], preferred_element_type=jnp.float32)
            for g in range(wanted // 8):
                points = []
                for b in range(RADIX):
                    at = b * wanted + g * 8
                    re, im = y[at : at + 8, :LANES], y[at : at + 8, LANES:]
                    c = back[b : b + 1, h * LANES : (h + 1) * LANES]
                    s = back[RADIX + b : RADIX + b + 1, h * LANES : (h + 1) * LANES]
                    if b == 0:
                        points.append((re, None))
                    elif b == RADIX // 2:
                        points.append((re * c - im * s, None))
                    else:
                        points.append((re * c - im * s, re * s + im * c))
                lags = gather8(points)
                for j in range(RADIX):
                    column = (j + RADIX // 2) % RADIX * width + h * LANES
                    out[a * wanted + g * 8 : a * wanted + g * 8 + 8, column : column + LANES] = lags[j]

    for copy in copies:
        copy.wait_send()


def solution(mesh):
    pairs, subs = mesh.shape["pairs"], mesh.shape["sub"]

    def body(raw_record, fir_taps, channel_ids, offsets, pair_table):
        rows, wins = raw_record.shape[0], offsets.shape[0]
        slots = pair_table.shape[0] // pairs
        block = 2 * rows
        leads = block // (2 * subs)
        unit = rows * wins
        assert unit == 8 and block == 8 and wins == 2
        assert rows == HALF
        units = pairs * 2 * subs
        vmem = pl.BlockSpec(memory_space=pltpu.VMEM)
        hbm = pl.BlockSpec(memory_space=pltpu.HBM)
        forward, twiddle, inverse, back = tables()
        total = leads * slots * block
        result = pl.pallas_call(
            functools.partial(kernel, (pairs, subs, rows, wins, slots, leads)),
            out_shape=jax.ShapeDtypeStruct((total, NF), jnp.float32),
            in_specs=[hbm] * 9,
            out_specs=vmem,
            scratch_shapes=[
                pltpu.VMEM((rows, raw_record.shape[1] + LANES), raw_record.dtype),
                pltpu.VMEM((1, TAPS), jnp.float32),
                pltpu.SMEM(channel_ids.shape, jnp.int32),
                pltpu.SMEM(offsets.shape, jnp.int32),
                pltpu.SMEM(pair_table.shape[::-1], jnp.int32),
                pltpu.VMEM(forward.shape, jnp.bfloat16),
                pltpu.VMEM(twiddle.shape, jnp.float32),
                pltpu.SemaphoreType.DMA((7,)),
                pltpu.VMEM((units, 2 * unit, NF // 2), jnp.bfloat16),
                pltpu.VMEM((8, LANES), jnp.float32),
                pltpu.VMEM((2 * LANES, LANES), jnp.float32),
                pltpu.VMEM((RADIX, total, 2 * LANES), jnp.bfloat16),
                pltpu.VMEM(inverse.shape, jnp.bfloat16),
                pltpu.VMEM(back.shape, jnp.float32),
                pltpu.SemaphoreType.DMA((2,)),
                pltpu.SemaphoreType.DMA((pairs,)),
                pltpu.SemaphoreType.DMA((pairs, subs)),
                pltpu.SemaphoreType.DMA((pairs, subs)),
                pltpu.SemaphoreType.DMA((units,)),
            ],
            compiler_params=pltpu.CompilerParams(
                collective_id=0, has_side_effects=True, vmem_limit_bytes=48*2**20),
        )(*[pltpu.with_memory_space_constraint(v, pltpu.HBM) for v in (raw_record, fir_taps.reshape(1, TAPS), channel_ids, offsets, pair_table.T,
          jnp.asarray(forward), jnp.asarray(twiddle), jnp.asarray(inverse), jnp.asarray(back))])
        return result.reshape(leads, slots, block, NF)

    return jax.shard_map(
        body,
        mesh=mesh,
        in_specs=(
            P(("groups", "pairs", "section"), "sub"),
            P(),
            P("groups"),
            P(("groups", "sub")),
            P("groups", None),
        ),
        out_specs=P(("section", "sub"), ("groups", "pairs"), None, None),
        check_vma=False,
    )
```

```python
import functools
import math

import jax
import jax.numpy as jnp
import numpy as np
from jax import lax
from jax.experimental import pallas as pl
from jax.experimental.pallas import tpu as pltpu
from jax.sharding import PartitionSpec as P

NF = 2048
TAPS = 64
DEC = 4
BAND = 64
LANES = 128
RADIX = 8
HALF = 4
FINE = LANES // DEC
REACH = 3
SPREAD = REACH + DEC - 1
PIECES = DEC * (NF // LANES)
MESH = pl.DeviceIdType.MESH


def round_bf16(values):
    return np.asarray(values).astype(jnp.bfloat16)


@functools.cache
def tables():
    kappa = np.arange(LANES)
    angle = 2 * np.pi * (kappa[:, None] * kappa[None, :] % (2 * LANES)) / (2 * LANES)
    c, s = np.cos(angle), np.sin(angle)
    dft = np.block([[c, -s], [s, c]])
    high = round_bf16(dft)
    low = round_bf16(dft - high.astype(np.float64))
    forward = np.concatenate([high, low], axis=0)
    n1 = (np.arange(8) // HALF * LANES)[:, None] + kappa[None, :]
    turn = 2 * np.pi * np.arange(RADIX)[:, None, None] * n1[None] / NF
    twiddle = np.stack([np.cos(turn), np.sin(turn)], axis=1).astype(np.float32)
    weight = 2.0 / math.sqrt(NF)
    cols = []
    for h in range(2):
        j1 = h * LANES + kappa
        theta = 2 * np.pi * (kappa[:, None] * j1[None, :] % (2 * LANES)) / (2 * LANES)
        c, s = weight * np.cos(theta), weight * np.sin(theta)
        cols.append(np.block([[c, s], [-s, c]]))
    inverse = round_bf16(np.concatenate(cols, axis=1))
    turn = 2 * np.pi * np.arange(RADIX)[:, None] * np.arange(2 * LANES)[None, :] / NF
    back = np.concatenate([np.cos(turn), np.sin(turn)], axis=0).astype(np.float32)
    return forward, twiddle, inverse, back


def spread8(d):
    c = math.sqrt(0.5)
    a = [d[i] + d[i + 4] for i in range(4)]
    m = [d[i] - d[i + 4] for i in range(4)]
    even, odd = a[0] + a[2], a[1] + a[3]
    u, v = c * (m[1] - m[3]), c * (m[1] + m[3])
    y1 = (m[0] + u, -m[2] - v)
    y3 = (m[0] - u, m[2] - v)
    y2 = (a[0] - a[2], a[3] - a[1])
    back = [(r, -i) for r, i in (y3, y2, y1)]
    return [(even + odd, None), y1, y2, y3, (even - odd, None)] + back


def gather8(x):
    c = math.sqrt(0.5)
    e0, o0 = x[0][0] + x[4][0], x[0][0] - x[4][0]
    p = [x[b][0] + x[8 - b][0] for b in (1, 2, 3)]
    q = [x[8 - b][1] - x[b][1] for b in (1, 2, 3)]
    pp, pm = p[0] + p[2], c * (p[0] - p[2])
    qm, qp = q[0] - q[2], c * (q[0] + q[2])
    ep, em = e0 + p[1], e0 - p[1]
    op, om = o0 + q[1], o0 - q[1]
    f, g = pm + qp, pm - qp
    return [ep + pp, op + f, em + qm, om - g, ep - pp, op - f, em - qm, om + g]


def kernel(sizes, raw_in, taps_in, ids_in, offs_in, table_in, forward_in, twiddle_in, inverse_in, back_in, out,
           raw, taps, ids, offs, table, forward, twiddle, in_sems,
           held, tapf, shifted, picks, orders, lhs, inv, back, late_sems, x_send, c_send, recv):
    pairs, subs, rows, wins, slots, leads = sizes
    unit = rows * wins
    block = 2 * rows
    p = lax.axis_index("pairs")
    sec = lax.axis_index("section")
    sub = lax.axis_index("sub")

    barrier = pltpu.get_barrier_semaphore()
    for dp in range(pairs):
        for d in range(subs):
            if dp or d:
                pl.semaphore_signal(
                    barrier, inc=1, device_id_type=MESH,
                    device_id={"pairs": lax.rem(p + dp, pairs), "sub": lax.rem(sub + d, subs)})
    pl.semaphore_signal(barrier, inc=1, device_id={"section": 1 - sec}, device_id_type=MESH)

    loads = [
        pltpu.make_async_copy(source, target, in_sems.at[i])
        for i, (source, target) in enumerate(
            ((taps_in, taps), (offs_in, offs), (raw_in, raw.at[:, pl.ds(0, raw_in.shape[1])]), (forward_in, forward),
             (twiddle_in, twiddle), (ids_in, ids), (table_in, table)))
    ]
    for load in loads:
        load.start()
    late = [
        pltpu.make_async_copy(source, target, late_sems.at[i])
        for i, (source, target) in enumerate(((inverse_in, inv), (back_in, back)))
    ]
    for load in late:
        load.start()
    tapf[...] = jnp.zeros_like(tapf)
    span = raw_in.shape[1]
    raw[:, span:] = jnp.zeros((rows, raw.shape[1] - span), raw.dtype)
    seg = lax.broadcasted_iota(jnp.int32, (2 * LANES, LANES), 0) % LANES // RADIX
    same = seg == lax.broadcasted_iota(jnp.int32, (2 * LANES, LANES), 1) // RADIX
    mean = jnp.where(same, 1.0 / BAND, 0.0).astype(jnp.bfloat16)
    sign = 1.0 - 2.0 * (lax.broadcasted_iota(jnp.int32, (8, LANES), 1) % 2).astype(jnp.float32)
    line8 = lax.broadcasted_iota(jnp.int32, (8, LANES), 0)
    top = line8 < HALF
    lane = lax.broadcasted_iota(jnp.int32, (FINE, LANES), 1)
    step = DEC * lax.broadcasted_iota(jnp.int32, (FINE, LANES), 0)
    for load in loads:
        load.wait()
    tapf[0:1, 0:TAPS] = taps[...]
    moved = jnp.broadcast_to(tapf[0:1, :], (8, LANES))
    for b in range(3):
        moved = jnp.where((line8 >> b) & 1 == 1, pltpu.roll(moved, 1 << b, 1), moved)
    for i in range(LANES // 8):
        ahead = pltpu.roll(moved, 8 * i, 1) if i else moved
        shifted[8 * i : 8 * i + 8, :] = ahead
        shifted[LANES + 8 * i : LANES + 8 * i + 8, :] = ahead
    blank = jnp.zeros((FINE, LANES), jnp.bfloat16)

    turned = []
    for w in range(wins):
        off = offs[w]
        first, rest = off // LANES, off % LANES
        rolled = shifted[pl.ds(rest, FINE, stride=DEC), :]
        highs, lows = [], []
        for s in range(REACH):
            t = lane + s * LANES - step - rest
            x = jnp.where((t >= 0) & (t < TAPS), rolled, 0.0)
            highs.append(x.astype(jnp.bfloat16))
            lows.append((x - highs[-1].astype(jnp.float32)).astype(jnp.bfloat16))
        cols = []
        for s in range(SPREAD):
            cols.append(jnp.concatenate(
                [part[s - f] if 0 <= s - f < REACH else blank for part in (highs, lows) for f in range(DEC)], axis=0))
        toeplitz = jnp.concatenate(cols, axis=1)
        seen = raw[:, pl.ds(first * LANES, (PIECES + SPREAD - DEC) * LANES)].astype(jnp.float32)
        piece = [seen[:, m * LANES : (m + 1) * LANES] for m in range(PIECES + SPREAD - DEC)]
        pair = [jnp.concatenate([piece[m], piece[m + DEC]], axis=0) for m in range(len(piece) - DEC)]
        data = jnp.concatenate(
            [jnp.concatenate([pair[s + 2 * DEC * n] for n in range(RADIX)], axis=0).astype(jnp.bfloat16)
             for s in range(SPREAD)], axis=1)
        total = lax.dot_general(data, toeplitz, (((1,), (1,)), ((), ())), preferred_element_type=jnp.float32)
        deci = (total[:, :LANES] + total[:, LANES:]).astype(jnp.bfloat16).astype(jnp.float32)
        parts = spread8([deci[8 * n : 8 * n + 8] for n in range(RADIX)])
        for b in range(RADIX):
            re, im = parts[b]
            c, s = twiddle[b, 0], twiddle[b, 1]
            if b == 0:
                re, im = re, jnp.zeros_like(re)
            elif im is None:
                re, im = re * c, -re * s
            else:
                re, im = re * c + im * s, im * c - re * s
            turned.append(jnp.concatenate([re, im], axis=1))
    z = jnp.concatenate(turned, axis=0)
    high = z.astype(jnp.bfloat16)
    low = (z - high.astype(jnp.float32)).astype(jnp.bfloat16)
    count_z = z.shape[0]
    both = jnp.dot(jnp.concatenate([high, low], axis=0), forward[: 2 * LANES, :], preferred_element_type=jnp.float32)
    both = both[:count_z] + both[count_z:] + jnp.dot(
        high, forward[2 * LANES :, :], preferred_element_type=jnp.float32)
    spectra = []
    power = None
    for b in range(RADIX):
        for part in range(2):
            lanes = slice(part * LANES, (part + 1) * LANES)
            u0 = both[b * 8 : b * 8 + 8, lanes]
            u1 = both[(RADIX + b) * 8 : (RADIX + b) * 8 + 8, lanes]
            near = jnp.where(top, u0, pltpu.roll(u1, HALF, 0))
            far = jnp.where(top, pltpu.roll(u0, HALF, 0), u1)
            x = near + sign * far
            spectra.append(x)
            power = x * x if power is None else power + x * x
    high = power.astype(jnp.bfloat16)
    low = (power - high.astype(jnp.float32)).astype(jnp.bfloat16)
    band = jnp.dot(jnp.concatenate([high, low], axis=1), mean, preferred_element_type=jnp.float32)
    gain = lax.rsqrt(band + 1e-06)
    mine = (p * 2 + sec) * subs + sub
    for b in range(RADIX):
        held[mine, :, b * LANES : (b + 1) * LANES] = jnp.concatenate(
            [spectra[2 * b] * gain, spectra[2 * b + 1] * gain], axis=0).astype(jnp.bfloat16)

    pl.semaphore_wait(barrier, pairs * subs)

    def send(slot, send_sem, device):
        return pltpu.make_async_remote_copy(
            src_ref=held.at[slot], dst_ref=held.at[slot], send_sem=send_sem,
            recv_sem=recv.at[slot], device_id=device, device_id_type=MESH)

    near = [p]
    for i in range(1, pairs):
        at = jnp.int32(0)
        for q in range(pairs):
            at = jnp.where(p == q, sorted(range(pairs), key=lambda t: (abs(t - q), t))[i], at)
        near.append(at)
    copies = []
    for dp in range(pairs - 1, -1, -1):
        for d in range(subs - 1, -1, -1):
            if not (dp or d):
                continue
            copies.append(send(mine, x_send.at[dp, d], {"pairs": near[dp], "sub": lax.rem(sub + d, subs)}))
            copies[-1].start()
    count = pairs * block
    tall = 2 * unit
    depth = pairs * 2 * subs * tall
    col = lax.broadcasted_iota(jnp.int32, (1, depth), 1)
    col_row = (col // (tall * subs)) * rows + col % rows
    col_id = jnp.full((1, depth), -1, jnp.int32)
    for i in range(count):
        col_id = jnp.where(col_row == i, ids[i], col_id)
    own = table[0, p * slots]
    for s in range(1, slots):
        own = jnp.maximum(own, table[0, p * slots + s])
    group = subs * tall
    line = lax.broadcasted_iota(jnp.int32, (2 * leads * group, 1), 0)
    lead = own * block + (sec * subs + sub) * leads + line // group % leads
    place = line // tall % subs * wins + line // rows % wins
    col_place = col // tall % subs * wins + col // rows % wins
    line_part, col_part = line // unit % 2, col // unit % 2
    crossing = line // (group * leads)
    chosen = (lead == col_id) & (place == col_place) & ((line_part + crossing) % 2 == col_part)
    value = jnp.where((crossing == 1) & (line_part == 1), -1.0, 1.0)
    pick = jnp.where(chosen, value, 0.0).astype(jnp.bfloat16)
    entry = lax.broadcasted_iota(jnp.int32, (slots * block, 1), 0)
    want = jnp.full((slots * block, 1), -1, jnp.int32)
    for s in range(slots):
        live = jnp.where(table[0, p * slots + s] >= 0, table[1, p * slots + s] * block, -block)
        want = jnp.where(entry // block == s, live + entry % block, want)
    order = jnp.where(want == col_id, 1.0 / (wins * subs), 0.0).astype(jnp.bfloat16)
    picks[...] = pick
    orders[...] = order

    for dp in range(pairs):
        for d in range(subs - 1, -1, -1):
            slot = (near[dp] * 2 + sec) * subs + lax.rem(sub + d, subs)
            if dp or d:
                send(slot, c_send.at[0, 0], {"section": 1 - sec}).wait_recv()
            copies.append(send(slot, c_send.at[dp, d], {"section": 1 - sec}))
            copies[-1].start()

    for load in late:
        load.wait()
    for dp in range(pairs):
        for d in range(subs):
            slot = (lax.rem(p + dp, pairs) * 2 + 1 - sec) * subs + lax.rem(sub + d, subs)
            send(slot, c_send.at[0, 0], {"section": 1 - sec}).wait_recv()

    width = 2 * LANES
    wanted = slots * block
    edge = jnp.where(lax.broadcasted_iota(jnp.int32, (wanted, LANES), 1) == 0, 0.5, 1.0)
    flats = [held[:, :, base * LANES : (base + 2) * LANES].reshape(depth, width) for base in range(0, RADIX, 2)]
    heads = [jnp.dot(picks[...], flat, preferred_element_type=jnp.float32).astype(jnp.bfloat16) for flat in flats]
    for base in range(0, RADIX, 2):
        for a in range(leads):
            for part in range(2):
                at = (part * leads + a) * group
                full = jnp.concatenate([heads[base // 2][at : at + group, :]] * (pairs * 2), axis=0)
                got = jnp.dot(orders[...], flats[base // 2] * full, preferred_element_type=jnp.float32)
                for h in range(2):
                    x = got[:, h * LANES : (h + 1) * LANES]
                    if base + h == 0:
                        x = x * edge
                    lhs[base + h, a * wanted : (a + 1) * wanted, part * LANES : (part + 1) * LANES] = x.astype(jnp.bfloat16)

    for h in range(2):
        for a in range(leads):
            x = lhs[:, a * wanted : (a + 1) * wanted, :].reshape(RADIX * wanted, width)
            y = jnp.dot(x, inv[:, h * width : (h + 1) * width], preferred_element_type=jnp.float32)
            for g in range(wanted // 8):
                points = []
                for b in range(RADIX):
                    at = b * wanted + g * 8
                    re, im = y[at : at + 8, :LANES], y[at : at + 8, LANES:]
                    c = back[b : b + 1, h * LANES : (h + 1) * LANES]
                    s = back[RADIX + b : RADIX + b + 1, h * LANES : (h + 1) * LANES]
                    if b == 0:
                        points.append((re, None))
                    elif b == RADIX // 2:
                        points.append((re * c - im * s, None))
                    else:
                        points.append((re * c - im * s, re * s + im * c))
                lags = gather8(points)
                for j in range(RADIX):
                    column = (j + RADIX // 2) % RADIX * width + h * LANES
                    out[a * wanted + g * 8 : a * wanted + g * 8 + 8, column : column + LANES] = lags[j]

    for copy in copies:
        copy.wait_send()


def solution(mesh):
    pairs, subs = mesh.shape["pairs"], mesh.shape["sub"]

    def body(raw_record, fir_taps, channel_ids, offsets, pair_table):
        rows, wins = raw_record.shape[0], offsets.shape[0]
        slots = pair_table.shape[0] // pairs
        block = 2 * rows
        leads = block // (2 * subs)
        unit = rows * wins
        assert unit == 8 and block == 8 and wins == 2
        assert rows == HALF
        units = pairs * 2 * subs
        vmem = pl.BlockSpec(memory_space=pltpu.VMEM)
        hbm = pl.BlockSpec(memory_space=pltpu.HBM)
        forward, twiddle, inverse, back = tables()
        total = leads * slots * block
        result = pl.pallas_call(
            functools.partial(kernel, (pairs, subs, rows, wins, slots, leads)),
            out_shape=jax.ShapeDtypeStruct((total, NF), jnp.float32),
            in_specs=[hbm] * 9,
            out_specs=vmem,
            scratch_shapes=[
                pltpu.VMEM((rows, raw_record.shape[1] + LANES), raw_record.dtype),
                pltpu.VMEM((1, TAPS), jnp.float32),
                pltpu.SMEM(channel_ids.shape, jnp.int32),
                pltpu.SMEM(offsets.shape, jnp.int32),
                pltpu.SMEM(pair_table.shape[::-1], jnp.int32),
                pltpu.VMEM(forward.shape, jnp.bfloat16),
                pltpu.VMEM(twiddle.shape, jnp.float32),
                pltpu.SemaphoreType.DMA((7,)),
                pltpu.VMEM((units, 2 * unit, NF // 2), jnp.bfloat16),
                pltpu.VMEM((8, LANES), jnp.float32),
                pltpu.VMEM((2 * LANES, LANES), jnp.float32),
                pltpu.VMEM((4 * leads * subs * unit, 2 * units * unit), jnp.bfloat16),
                pltpu.VMEM((slots * block, 2 * units * unit), jnp.bfloat16),
                pltpu.VMEM((RADIX, total, 2 * LANES), jnp.bfloat16),
                pltpu.VMEM(inverse.shape, jnp.bfloat16),
                pltpu.VMEM(back.shape, jnp.float32),
                pltpu.SemaphoreType.DMA((2,)),
                pltpu.SemaphoreType.DMA((pairs, subs)),
                pltpu.SemaphoreType.DMA((pairs, subs)),
                pltpu.SemaphoreType.DMA((units,)),
            ],
            compiler_params=pltpu.CompilerParams(
                collective_id=0, has_side_effects=True, vmem_limit_bytes=48*2**20),
        )(*[pltpu.with_memory_space_constraint(v, pltpu.HBM) for v in (raw_record, fir_taps.reshape(1, TAPS), channel_ids, offsets, pair_table.T,
          jnp.asarray(forward), jnp.asarray(twiddle), jnp.asarray(inverse), jnp.asarray(back))])
        return result.reshape(leads, slots, block, NF)

    return jax.shard_map(
        body,
        mesh=mesh,
        in_specs=(
            P(("groups", "pairs", "section"), "sub"),
            P(),
            P("groups"),
            P(("groups", "sub")),
            P("groups", None),
        ),
        out_specs=P(("section", "sub"), ("groups", "pairs"), None, None),
        check_vma=False,
    )
```

```python
import functools
import math

import jax
import jax.numpy as jnp
import numpy as np
from jax import lax
from jax.experimental import pallas as pl
from jax.experimental.pallas import tpu as pltpu
from jax.sharding import PartitionSpec as P

NF = 2048
TAPS = 64
DEC = 4
BAND = 64
LANES = 128
RADIX = 8
HALF = 4
FINE = LANES // DEC
REACH = 3
SPREAD = REACH + DEC - 1
PIECES = DEC * (NF // LANES)
MESH = pl.DeviceIdType.MESH


def round_bf16(values):
    return np.asarray(values).astype(jnp.bfloat16)


@functools.cache
def tables():
    kappa = np.arange(LANES)
    angle = 2 * np.pi * (kappa[:, None] * kappa[None, :] % (2 * LANES)) / (2 * LANES)
    c, s = np.cos(angle), np.sin(angle)
    dft = np.block([[c, -s], [s, c]])
    high = round_bf16(dft)
    low = round_bf16(dft - high.astype(np.float64))
    forward = np.concatenate([high, low], axis=0)
    n1 = (np.arange(8) // HALF * LANES)[:, None] + kappa[None, :]
    turn = 2 * np.pi * np.arange(RADIX)[:, None, None] * n1[None] / NF
    twiddle = np.stack([np.cos(turn), np.sin(turn)], axis=1).astype(np.float32)
    weight = 2.0 / math.sqrt(NF)
    cols = []
    for h in range(2):
        j1 = h * LANES + kappa
        theta = 2 * np.pi * (kappa[:, None] * j1[None, :] % (2 * LANES)) / (2 * LANES)
        c, s = weight * np.cos(theta), weight * np.sin(theta)
        cols.append(np.block([[c, s], [-s, c]]))
    inverse = round_bf16(np.concatenate(cols, axis=1))
    turn = 2 * np.pi * np.arange(RADIX)[:, None] * np.arange(2 * LANES)[None, :] / NF
    back = np.concatenate([np.cos(turn), np.sin(turn)], axis=0).astype(np.float32)
    return forward, twiddle, inverse, back


def spread8(d):
    c = math.sqrt(0.5)
    a = [d[i] + d[i + 4] for i in range(4)]
    m = [d[i] - d[i + 4] for i in range(4)]
    even, odd = a[0] + a[2], a[1] + a[3]
    u, v = c * (m[1] - m[3]), c * (m[1] + m[3])
    y1 = (m[0] + u, -m[2] - v)
    y3 = (m[0] - u, m[2] - v)
    y2 = (a[0] - a[2], a[3] - a[1])
    back = [(r, -i) for r, i in (y3, y2, y1)]
    return [(even + odd, None), y1, y2, y3, (even - odd, None)] + back


def gather8(x):
    c = math.sqrt(0.5)
    e0, o0 = x[0][0] + x[4][0], x[0][0] - x[4][0]
    p = [x[b][0] + x[8 - b][0] for b in (1, 2, 3)]
    q = [x[8 - b][1] - x[b][1] for b in (1, 2, 3)]
    pp, pm = p[0] + p[2], c * (p[0] - p[2])
    qm, qp = q[0] - q[2], c * (q[0] + q[2])
    ep, em = e0 + p[1], e0 - p[1]
    op, om = o0 + q[1], o0 - q[1]
    f, g = pm + qp, pm - qp
    return [ep + pp, op + f, em + qm, om - g, ep - pp, op - f, em - qm, om + g]


def kernel(sizes, raw_in, taps_in, ids_in, offs_in, table_in, forward_in, twiddle_in, inverse_in, back_in, out,
           raw, taps, ids, offs, table, forward, twiddle, in_sems,
           held, tapf, shifted, picks, orders, lhs, inv, back, late_sems, x_send, c_send, swap, recv):
    pairs, subs, rows, wins, slots, leads = sizes
    unit = rows * wins
    block = 2 * rows
    p = lax.axis_index("pairs")
    sec = lax.axis_index("section")
    sub = lax.axis_index("sub")

    loads = [
        pltpu.make_async_copy(source, target, in_sems.at[i])
        for i, (source, target) in enumerate(
            ((taps_in, taps), (offs_in, offs), (raw_in, raw.at[:, pl.ds(0, raw_in.shape[1])]), (forward_in, forward),
             (twiddle_in, twiddle), (ids_in, ids), (table_in, table)))
    ]
    for load in loads:
        load.start()
    late = [
        pltpu.make_async_copy(source, target, late_sems.at[i])
        for i, (source, target) in enumerate(((inverse_in, inv), (back_in, back)))
    ]
    for load in late:
        load.start()
    barrier = pltpu.get_barrier_semaphore()
    for dp in range(pairs):
        for d in range(subs):
            if dp or d:
                pl.semaphore_signal(
                    barrier, inc=1, device_id_type=MESH,
                    device_id={"pairs": lax.rem(p + dp, pairs), "sub": lax.rem(sub + d, subs)})
    pl.semaphore_signal(barrier, inc=1, device_id={"section": 1 - sec}, device_id_type=MESH)

    tapf[...] = jnp.zeros_like(tapf)
    span = raw_in.shape[1]
    raw[:, span:] = jnp.zeros((rows, raw.shape[1] - span), raw.dtype)
    seg = lax.broadcasted_iota(jnp.int32, (2 * LANES, LANES), 0) % LANES // RADIX
    same = seg == lax.broadcasted_iota(jnp.int32, (2 * LANES, LANES), 1) // RADIX
    mean = jnp.where(same, 1.0 / BAND, 0.0).astype(jnp.bfloat16)
    sign = 1.0 - 2.0 * (lax.broadcasted_iota(jnp.int32, (8, LANES), 1) % 2).astype(jnp.float32)
    line8 = lax.broadcasted_iota(jnp.int32, (8, LANES), 0)
    top = line8 < HALF
    lane = lax.broadcasted_iota(jnp.int32, (FINE, LANES), 1)
    step = DEC * lax.broadcasted_iota(jnp.int32, (FINE, LANES), 0)
    for load in loads:
        load.wait()
    tapf[0:1, 0:TAPS] = taps[...]
    moved = jnp.broadcast_to(tapf[0:1, :], (8, LANES))
    for b in range(3):
        moved = jnp.where((line8 >> b) & 1 == 1, pltpu.roll(moved, 1 << b, 1), moved)
    for i in range(LANES // 8):
        ahead = pltpu.roll(moved, 8 * i, 1) if i else moved
        shifted[8 * i : 8 * i + 8, :] = ahead
        shifted[LANES + 8 * i : LANES + 8 * i + 8, :] = ahead
    blank = jnp.zeros((FINE, LANES), jnp.bfloat16)

    turned = []
    for w in range(wins):
        off = offs[w]
        first, rest = off // LANES, off % LANES
        rolled = shifted[pl.ds(rest, FINE, stride=DEC), :]
        highs, lows = [], []
        for s in range(REACH):
            t = lane + s * LANES - step - rest
            x = jnp.where((t >= 0) & (t < TAPS), rolled, 0.0)
            highs.append(x.astype(jnp.bfloat16))
            lows.append((x - highs[-1].astype(jnp.float32)).astype(jnp.bfloat16))
        cols = []
        for s in range(SPREAD):
            cols.append(jnp.concatenate(
                [part[s - f] if 0 <= s - f < REACH else blank for part in (highs, lows) for f in range(DEC)], axis=0))
        toeplitz = jnp.concatenate(cols, axis=1)
        seen = raw[:, pl.ds(first * LANES, (PIECES + SPREAD - DEC) * LANES)].astype(jnp.float32)
        piece = [seen[:, m * LANES : (m + 1) * LANES] for m in range(PIECES + SPREAD - DEC)]
        pair = [jnp.concatenate([piece[m], piece[m + DEC]], axis=0) for m in range(len(piece) - DEC)]
        data = jnp.concatenate(
            [jnp.concatenate([pair[s + 2 * DEC * n] for n in range(RADIX)], axis=0).astype(jnp.bfloat16)
             for s in range(SPREAD)], axis=1)
        total = lax.dot_general(data, toeplitz, (((1,), (1,)), ((), ())), preferred_element_type=jnp.float32)
        deci = (total[:, :LANES] + total[:, LANES:]).astype(jnp.bfloat16).astype(jnp.float32)
        parts = spread8([deci[8 * n : 8 * n + 8] for n in range(RADIX)])
        for b in range(RADIX):
            re, im = parts[b]
            c, s = twiddle[b, 0], twiddle[b, 1]
            if b == 0:
                re, im = re, jnp.zeros_like(re)
            elif im is None:
                re, im = re * c, -re * s
            else:
                re, im = re * c + im * s, im * c - re * s
            turned.append(jnp.concatenate([re, im], axis=1))
    z = jnp.concatenate(turned, axis=0)
    high = z.astype(jnp.bfloat16)
    low = (z - high.astype(jnp.float32)).astype(jnp.bfloat16)
    count_z = z.shape[0]
    both = jnp.dot(jnp.concatenate([high, low], axis=0), forward[: 2 * LANES, :], preferred_element_type=jnp.float32)
    both = both[:count_z] + both[count_z:] + jnp.dot(
        high, forward[2 * LANES :, :], preferred_element_type=jnp.float32)
    spectra = []
    power = None
    for b in range(RADIX):
        for part in range(2):
            lanes = slice(part * LANES, (part + 1) * LANES)
            u0 = both[b * 8 : b * 8 + 8, lanes]
            u1 = both[(RADIX + b) * 8 : (RADIX + b) * 8 + 8, lanes]
            near = jnp.where(top, u0, pltpu.roll(u1, HALF, 0))
            far = jnp.where(top, pltpu.roll(u0, HALF, 0), u1)
            x = near + sign * far
            spectra.append(x)
            power = x * x if power is None else power + x * x
    high = power.astype(jnp.bfloat16)
    low = (power - high.astype(jnp.float32)).astype(jnp.bfloat16)
    band = jnp.dot(jnp.concatenate([high, low], axis=1), mean, preferred_element_type=jnp.float32)
    gain = lax.rsqrt(band + 1e-06)
    mine = (p * 2 + sec) * subs + sub
    for b in range(RADIX):
        held[mine, :, b * LANES : (b + 1) * LANES] = jnp.concatenate(
            [spectra[2 * b] * gain, spectra[2 * b + 1] * gain], axis=0).astype(jnp.bfloat16)

    pl.semaphore_wait(barrier, pairs * subs)

    def send(slot, send_sem, device, arrival):
        return pltpu.make_async_remote_copy(
            src_ref=held.at[slot], dst_ref=held.at[slot], send_sem=send_sem,
            recv_sem=arrival, device_id=device, device_id_type=MESH)

    near = [p]
    for i in range(1, pairs):
        at = jnp.int32(0)
        for q in range(pairs):
            at = jnp.where(p == q, sorted(range(pairs), key=lambda t: (abs(t - q), t))[i], at)
        near.append(at)
    here = p * subs + sub
    for dp in range(pairs - 1, -1, -1):
        for d in range(subs - 1, -1, -1):
            if dp or d:
                send(mine, x_send, {"pairs": near[dp], "sub": lax.rem(sub + d, subs)}, recv.at[here]).start()

    count = pairs * block
    tall = 2 * unit
    depth = pairs * 2 * subs * tall
    col = lax.broadcasted_iota(jnp.int32, (1, depth), 1)
    col_row = (col // (tall * subs)) * rows + col % rows
    col_id = jnp.full((1, depth), -1, jnp.int32)
    for i in range(count):
        col_id = jnp.where(col_row == i, ids[i], col_id)
    own = table[0, p * slots]
    for s in range(1, slots):
        own = jnp.maximum(own, table[0, p * slots + s])
    group = subs * tall
    line = lax.broadcasted_iota(jnp.int32, (2 * leads * group, 1), 0)
    lead = own * block + (sec * subs + sub) * leads + line // group % leads
    place = line // tall % subs * wins + line // rows % wins
    col_place = col // tall % subs * wins + col // rows % wins
    line_part, col_part = line // unit % 2, col // unit % 2
    crossing = line // (group * leads)
    chosen = (lead == col_id) & (place == col_place) & ((line_part + crossing) % 2 == col_part)
    value = jnp.where((crossing == 1) & (line_part == 1), -1.0, 1.0)
    pick = jnp.where(chosen, value, 0.0).astype(jnp.bfloat16)
    entry = lax.broadcasted_iota(jnp.int32, (slots * block, 1), 0)
    want = jnp.full((slots * block, 1), -1, jnp.int32)
    for s in range(slots):
        live = jnp.where(table[0, p * slots + s] >= 0, table[1, p * slots + s] * block, -block)
        want = jnp.where(entry // block == s, live + entry % block, want)
    order = jnp.where(want == col_id, 1.0 / (wins * subs), 0.0).astype(jnp.bfloat16)
    picks[...] = pick
    orders[...] = order

    for dp in range(pairs):
        for d in range(subs - 1, -1, -1):
            across = lax.rem(sub + d, subs)
            slot = (near[dp] * 2 + sec) * subs + across
            if dp or d:
                send(slot, x_send, {"section": 1 - sec}, recv.at[near[dp] * subs + across]).wait_recv()
            send(slot, c_send, {"section": 1 - sec}, swap).start()

    for load in late:
        load.wait()
    half = pairs * subs
    send(pl.ds(0, half), c_send, {"section": 1 - sec}, swap).wait_recv()

    width = 2 * LANES
    wanted = slots * block
    edge = jnp.where(lax.broadcasted_iota(jnp.int32, (wanted, LANES), 1) == 0, 0.5, 1.0)
    flats = [held[:, :, base * LANES : (base + 2) * LANES].reshape(depth, width) for base in range(0, RADIX, 2)]
    heads = [jnp.dot(picks[...], flat, preferred_element_type=jnp.float32).astype(jnp.bfloat16) for flat in flats]
    for base in range(0, RADIX, 2):
        for a in range(leads):
            for part in range(2):
                at = (part * leads + a) * group
                full = jnp.concatenate([heads[base // 2][at : at + group, :]] * (pairs * 2), axis=0)
                got = jnp.dot(orders[...], flats[base // 2] * full, preferred_element_type=jnp.float32)
                for h in range(2):
                    x = got[:, h * LANES : (h + 1) * LANES]
                    if base + h == 0:
                        x = x * edge
                    lhs[base + h, a * wanted : (a + 1) * wanted, part * LANES : (part + 1) * LANES] = x.astype(jnp.bfloat16)

    for h in range(2):
        for a in range(leads):
            x = lhs[:, a * wanted : (a + 1) * wanted, :].reshape(RADIX * wanted, width)
            y = jnp.dot(x, inv[:, h * width : (h + 1) * width], preferred_element_type=jnp.float32)
            for g in range(wanted // 8):
                points = []
                for b in range(RADIX):
                    at = b * wanted + g * 8
                    re, im = y[at : at + 8, :LANES], y[at : at + 8, LANES:]
                    c = back[b : b + 1, h * LANES : (h + 1) * LANES]
                    s = back[RADIX + b : RADIX + b + 1, h * LANES : (h + 1) * LANES]
                    if b == 0:
                        points.append((re, None))
                    elif b == RADIX // 2:
                        points.append((re * c - im * s, None))
                    else:
                        points.append((re * c - im * s, re * s + im * c))
                lags = gather8(points)
                for j in range(RADIX):
                    column = (j + RADIX // 2) % RADIX * width + h * LANES
                    out[a * wanted + g * 8 : a * wanted + g * 8 + 8, column : column + LANES] = lags[j]

    send(pl.ds(0, half - 1), x_send, {"section": 1 - sec}, swap).wait_send()
    send(pl.ds(0, half), c_send, {"section": 1 - sec}, swap).wait_send()


def solution(mesh):
    pairs, subs = mesh.shape["pairs"], mesh.shape["sub"]

    def body(raw_record, fir_taps, channel_ids, offsets, pair_table):
        rows, wins = raw_record.shape[0], offsets.shape[0]
        slots = pair_table.shape[0] // pairs
        block = 2 * rows
        leads = block // (2 * subs)
        unit = rows * wins
        assert unit == 8 and block == 8 and wins == 2
        assert rows == HALF
        units = pairs * 2 * subs
        vmem = pl.BlockSpec(memory_space=pltpu.VMEM)
        hbm = pl.BlockSpec(memory_space=pltpu.HBM)
        forward, twiddle, inverse, back = tables()
        total = leads * slots * block
        result = pl.pallas_call(
            functools.partial(kernel, (pairs, subs, rows, wins, slots, leads)),
            out_shape=jax.ShapeDtypeStruct((total, NF), jnp.float32),
            in_specs=[hbm] * 9,
            out_specs=vmem,
            scratch_shapes=[
                pltpu.VMEM((rows, raw_record.shape[1] + LANES), raw_record.dtype),
                pltpu.VMEM((1, TAPS), jnp.float32),
                pltpu.SMEM(channel_ids.shape, jnp.int32),
                pltpu.SMEM(offsets.shape, jnp.int32),
                pltpu.SMEM(pair_table.shape[::-1], jnp.int32),
                pltpu.VMEM(forward.shape, jnp.bfloat16),
                pltpu.VMEM(twiddle.shape, jnp.float32),
                pltpu.SemaphoreType.DMA((7,)),
                pltpu.VMEM((units, 2 * unit, NF // 2), jnp.bfloat16),
                pltpu.VMEM((8, LANES), jnp.float32),
                pltpu.VMEM((2 * LANES, LANES), jnp.float32),
                pltpu.VMEM((4 * leads * subs * unit, 2 * units * unit), jnp.bfloat16),
                pltpu.VMEM((slots * block, 2 * units * unit), jnp.bfloat16),
                pltpu.VMEM((RADIX, total, 2 * LANES), jnp.bfloat16),
                pltpu.VMEM(inverse.shape, jnp.bfloat16),
                pltpu.VMEM(back.shape, jnp.float32),
                pltpu.SemaphoreType.DMA((2,)),
                pltpu.SemaphoreType.DMA,
                pltpu.SemaphoreType.DMA,
                pltpu.SemaphoreType.DMA,
                pltpu.SemaphoreType.DMA((pairs * subs,)),
            ],
            compiler_params=pltpu.CompilerParams(
                collective_id=0, has_side_effects=True, vmem_limit_bytes=48*2**20),
        )(*[pltpu.with_memory_space_constraint(v, pltpu.HBM) for v in (raw_record, fir_taps.reshape(1, TAPS), channel_ids, offsets, pair_table.T,
          jnp.asarray(forward), jnp.asarray(twiddle), jnp.asarray(inverse), jnp.asarray(back))])
        return result.reshape(leads, slots, block, NF)

    return jax.shard_map(
        body,
        mesh=mesh,
        in_specs=(
            P(("groups", "pairs", "section"), "sub"),
            P(),
            P("groups"),
            P(("groups", "sub")),
            P("groups", None),
        ),
        out_specs=P(("section", "sub"), ("groups", "pairs"), None, None),
        check_vma=False,
    )
```

```python
import functools
import math

import jax
import jax.numpy as jnp
import numpy as np
from jax import lax
from jax.experimental import pallas as pl
from jax.experimental.pallas import tpu as pltpu
from jax.sharding import PartitionSpec as P

NF = 2048
TAPS = 64
DEC = 4
BAND = 64
LANES = 128
RADIX = 8
HALF = 4
FINE = LANES // DEC
REACH = 3
SPREAD = REACH + DEC - 1
PIECES = DEC * (NF // LANES)
MESH = pl.DeviceIdType.MESH


def round_bf16(values):
    return np.asarray(values).astype(jnp.bfloat16)


@functools.cache
def tables():
    kappa = np.arange(LANES)
    angle = 2 * np.pi * (kappa[:, None] * kappa[None, :] % (2 * LANES)) / (2 * LANES)
    c, s = np.cos(angle), np.sin(angle)
    dft = np.block([[c, -s], [s, c]])
    high = round_bf16(dft)
    low = round_bf16(dft - high.astype(np.float64))
    forward = np.concatenate([high, low], axis=0)
    n1 = (np.arange(8) // HALF * LANES)[:, None] + kappa[None, :]
    turn = 2 * np.pi * np.arange(RADIX)[:, None, None] * n1[None] / NF
    twiddle = np.stack([np.cos(turn), np.sin(turn)], axis=1).astype(np.float32)
    weight = 2.0 / math.sqrt(NF)
    cols = []
    for h in range(2):
        j1 = h * LANES + kappa
        theta = 2 * np.pi * (kappa[:, None] * j1[None, :] % (2 * LANES)) / (2 * LANES)
        c, s = weight * np.cos(theta), weight * np.sin(theta)
        cols.append(np.block([[c, s], [-s, c]]))
    inverse = round_bf16(np.concatenate(cols, axis=1))
    turn = 2 * np.pi * np.arange(RADIX)[:, None] * np.arange(2 * LANES)[None, :] / NF
    back = np.concatenate([np.cos(turn), np.sin(turn)], axis=0).astype(np.float32)
    return forward, twiddle, inverse, back


def spread8(d):
    c = math.sqrt(0.5)
    a = [d[i] + d[i + 4] for i in range(4)]
    m = [d[i] - d[i + 4] for i in range(4)]
    even, odd = a[0] + a[2], a[1] + a[3]
    u, v = c * (m[1] - m[3]), c * (m[1] + m[3])
    y1 = (m[0] + u, -m[2] - v)
    y3 = (m[0] - u, m[2] - v)
    y2 = (a[0] - a[2], a[3] - a[1])
    back = [(r, -i) for r, i in (y3, y2, y1)]
    return [(even + odd, None), y1, y2, y3, (even - odd, None)] + back


def gather8(x):
    c = math.sqrt(0.5)
    e0, o0 = x[0][0] + x[4][0], x[0][0] - x[4][0]
    p = [x[b][0] + x[8 - b][0] for b in (1, 2, 3)]
    q = [x[8 - b][1] - x[b][1] for b in (1, 2, 3)]
    pp, pm = p[0] + p[2], c * (p[0] - p[2])
    qm, qp = q[0] - q[2], c * (q[0] + q[2])
    ep, em = e0 + p[1], e0 - p[1]
    op, om = o0 + q[1], o0 - q[1]
    f, g = pm + qp, pm - qp
    return [ep + pp, op + f, em + qm, om - g, ep - pp, op - f, em - qm, om + g]


def kernel(sizes, raw_in, taps_in, ids_in, offs_in, table_in, forward_in, twiddle_in, inverse_in, back_in, out,
           raw, taps, ids, offs, table, forward, twiddle, in_sems,
           held, tapf, shifted, picks, orders, lhs, inv, back, late_sems, x_send, c_send, swap, recv):
    pairs, subs, rows, wins, slots, leads = sizes
    unit = rows * wins
    block = 2 * rows
    p = lax.axis_index("pairs")
    sec = lax.axis_index("section")
    sub = lax.axis_index("sub")

    loads = [
        pltpu.make_async_copy(source, target, in_sems.at[i])
        for i, (source, target) in enumerate(
            ((taps_in, taps), (offs_in, offs), (raw_in, raw.at[:, pl.ds(0, raw_in.shape[1])]), (forward_in, forward),
             (twiddle_in, twiddle), (ids_in, ids), (table_in, table)))
    ]
    for load in loads:
        load.start()
    late = [
        pltpu.make_async_copy(source, target, late_sems.at[i])
        for i, (source, target) in enumerate(((inverse_in, inv), (back_in, back)))
    ]
    for load in late:
        load.start()
    barrier = pltpu.get_barrier_semaphore()
    for dp in range(pairs):
        for d in range(subs):
            if dp or d:
                pl.semaphore_signal(
                    barrier, inc=1, device_id_type=MESH,
                    device_id={"pairs": lax.rem(p + dp, pairs), "sub": lax.rem(sub + d, subs)})
    pl.semaphore_signal(barrier, inc=1, device_id={"section": 1 - sec}, device_id_type=MESH)

    tapf[...] = jnp.zeros_like(tapf)
    span = raw_in.shape[1]
    raw[:, span:] = jnp.zeros((rows, raw.shape[1] - span), raw.dtype)
    seg = lax.broadcasted_iota(jnp.int32, (2 * LANES, LANES), 0) % LANES // RADIX
    same = seg == lax.broadcasted_iota(jnp.int32, (2 * LANES, LANES), 1) // RADIX
    mean = jnp.where(same, 1.0 / BAND, 0.0).astype(jnp.bfloat16)
    sign = 1.0 - 2.0 * (lax.broadcasted_iota(jnp.int32, (8, LANES), 1) % 2).astype(jnp.float32)
    line8 = lax.broadcasted_iota(jnp.int32, (8, LANES), 0)
    top = line8 < HALF
    lane = lax.broadcasted_iota(jnp.int32, (FINE, LANES), 1)
    step = DEC * lax.broadcasted_iota(jnp.int32, (FINE, LANES), 0)
    for load in loads:
        load.wait()
    tapf[0:1, 0:TAPS] = taps[...]
    moved = jnp.broadcast_to(tapf[0:1, :], (8, LANES))
    for b in range(3):
        moved = jnp.where((line8 >> b) & 1 == 1, pltpu.roll(moved, 1 << b, 1), moved)
    for i in range(LANES // 8):
        ahead = pltpu.roll(moved, 8 * i, 1) if i else moved
        shifted[8 * i : 8 * i + 8, :] = ahead
        shifted[LANES + 8 * i : LANES + 8 * i + 8, :] = ahead
    blank = jnp.zeros((FINE, LANES), jnp.bfloat16)

    turned = []
    for w in range(wins):
        off = offs[w]
        first, rest = off // LANES, off % LANES
        rolled = shifted[pl.ds(rest, FINE, stride=DEC), :]
        highs, lows = [], []
        for s in range(REACH):
            t = lane + s * LANES - step - rest
            x = jnp.where((t >= 0) & (t < TAPS), rolled, 0.0)
            highs.append(x.astype(jnp.bfloat16))
            lows.append((x - highs[-1].astype(jnp.float32)).astype(jnp.bfloat16))
        cols = []
        for s in range(SPREAD):
            cols.append(jnp.concatenate(
                [part[s - f] if 0 <= s - f < REACH else blank for part in (highs, lows) for f in range(DEC)], axis=0))
        toeplitz = jnp.concatenate(cols, axis=1)
        seen = raw[:, pl.ds(first * LANES, (PIECES + SPREAD - DEC) * LANES)].astype(jnp.float32)
        piece = [seen[:, m * LANES : (m + 1) * LANES] for m in range(PIECES + SPREAD - DEC)]
        pair = [jnp.concatenate([piece[m], piece[m + DEC]], axis=0) for m in range(len(piece) - DEC)]
        data = jnp.concatenate(
            [jnp.concatenate([pair[s + 2 * DEC * n] for n in range(RADIX)], axis=0).astype(jnp.bfloat16)
             for s in range(SPREAD)], axis=1)
        total = lax.dot_general(data, toeplitz, (((1,), (1,)), ((), ())), preferred_element_type=jnp.float32)
        deci = (total[:, :LANES] + total[:, LANES:]).astype(jnp.bfloat16).astype(jnp.float32)
        parts = spread8([deci[8 * n : 8 * n + 8] for n in range(RADIX)])
        for b in range(RADIX):
            re, im = parts[b]
            c, s = twiddle[b, 0], twiddle[b, 1]
            if b == 0:
                re, im = re, jnp.zeros_like(re)
            elif im is None:
                re, im = re * c, -re * s
            else:
                re, im = re * c + im * s, im * c - re * s
            turned.append(jnp.concatenate([re, im], axis=1))
    z = jnp.concatenate(turned, axis=0)
    high = z.astype(jnp.bfloat16)
    low = (z - high.astype(jnp.float32)).astype(jnp.bfloat16)
    count_z = z.shape[0]
    both = jnp.dot(jnp.concatenate([high, low], axis=0), forward[: 2 * LANES, :], preferred_element_type=jnp.float32)
    both = both[:count_z] + both[count_z:] + jnp.dot(
        high, forward[2 * LANES :, :], preferred_element_type=jnp.float32)
    spectra = []
    power = None
    for b in range(RADIX):
        for part in range(2):
            lanes = slice(part * LANES, (part + 1) * LANES)
            u0 = both[b * 8 : b * 8 + 8, lanes]
            u1 = both[(RADIX + b) * 8 : (RADIX + b) * 8 + 8, lanes]
            near = jnp.where(top, u0, pltpu.roll(u1, HALF, 0))
            far = jnp.where(top, pltpu.roll(u0, HALF, 0), u1)
            x = near + sign * far
            spectra.append(x)
            power = x * x if power is None else power + x * x
    high = power.astype(jnp.bfloat16)
    low = (power - high.astype(jnp.float32)).astype(jnp.bfloat16)
    band = jnp.dot(jnp.concatenate([high, low], axis=1), mean, preferred_element_type=jnp.float32)
    gain = lax.rsqrt(band + 1e-06)
    mine = (p * 2 + sec) * subs + sub
    for b in range(RADIX):
        held[mine, :, b * LANES : (b + 1) * LANES] = jnp.concatenate(
            [spectra[2 * b] * gain, spectra[2 * b + 1] * gain], axis=0).astype(jnp.bfloat16)

    pl.semaphore_wait(barrier, pairs * subs)

    def send(slot, send_sem, device, arrival):
        return pltpu.make_async_remote_copy(
            src_ref=held.at[slot], dst_ref=held.at[slot], send_sem=send_sem,
            recv_sem=arrival, device_id=device, device_id_type=MESH)

    near = [p]
    for i in range(1, pairs):
        at = jnp.int32(0)
        for q in range(pairs):
            at = jnp.where(p == q, sorted(range(pairs), key=lambda t: (abs(t - q), t))[i], at)
        near.append(at)
    here = p * subs + sub
    for dp in range(pairs - 1, -1, -1):
        for d in range(subs - 1, -1, -1):
            if dp or d:
                send(mine, x_send, {"pairs": near[dp], "sub": lax.rem(sub + d, subs)}, recv.at[here]).start()

    count = pairs * block
    tall = 2 * unit
    depth = pairs * 2 * subs * tall
    col = lax.broadcasted_iota(jnp.int32, (1, depth), 1)
    col_row = (col // (tall * subs)) * rows + col % rows
    col_id = jnp.full((1, depth), -1, jnp.int32)
    for i in range(count):
        col_id = jnp.where(col_row == i, ids[i], col_id)
    own = table[0, p * slots]
    for s in range(1, slots):
        own = jnp.maximum(own, table[0, p * slots + s])
    group = subs * tall
    line = lax.broadcasted_iota(jnp.int32, (2 * leads * group, 1), 0)
    lead = own * block + (sec * subs + sub) * leads + line // group % leads
    place = line // tall % subs * wins + line // rows % wins
    col_place = col // tall % subs * wins + col // rows % wins
    line_part, col_part = line // unit % 2, col // unit % 2
    crossing = line // (group * leads)
    chosen = (lead == col_id) & (place == col_place) & ((line_part + crossing) % 2 == col_part)
    value = jnp.where((crossing == 1) & (line_part == 1), -1.0, 1.0)
    pick = jnp.where(chosen, value, 0.0).astype(jnp.bfloat16)
    entry = lax.broadcasted_iota(jnp.int32, (slots * block, 1), 0)
    want = jnp.full((slots * block, 1), -1, jnp.int32)
    for s in range(slots):
        live = jnp.where(table[0, p * slots + s] >= 0, table[1, p * slots + s] * block, -block)
        want = jnp.where(entry // block == s, live + entry % block, want)
    order = jnp.where(want == col_id, 1.0 / (wins * subs), 0.0).astype(jnp.bfloat16)
    picks[...] = pick
    orders[...] = order

    for dp in range(pairs):
        for d in (range(subs) if dp == pairs - 1 else range(subs - 1, -1, -1)):
            across = lax.rem(sub + d, subs)
            slot = (near[dp] * 2 + sec) * subs + across
            if dp or d:
                send(slot, x_send, {"section": 1 - sec}, recv.at[near[dp] * subs + across]).wait_recv()
            send(slot, c_send, {"section": 1 - sec}, swap).start()

    for load in late:
        load.wait()
    half = pairs * subs
    send(pl.ds(0, half), c_send, {"section": 1 - sec}, swap).wait_recv()

    width = 2 * LANES
    wanted = slots * block
    edge = jnp.where(lax.broadcasted_iota(jnp.int32, (wanted, LANES), 1) == 0, 0.5, 1.0)
    flats = [held[:, :, base * LANES : (base + 2) * LANES].reshape(depth, width) for base in range(0, RADIX, 2)]
    heads = [jnp.dot(picks[...], flat, preferred_element_type=jnp.float32).astype(jnp.bfloat16) for flat in flats]
    for base in range(0, RADIX, 2):
        for a in range(leads):
            for part in range(2):
                at = (part * leads + a) * group
                full = jnp.concatenate([heads[base // 2][at : at + group, :]] * (pairs * 2), axis=0)
                got = jnp.dot(orders[...], flats[base // 2] * full, preferred_element_type=jnp.float32)
                for h in range(2):
                    x = got[:, h * LANES : (h + 1) * LANES]
                    if base + h == 0:
                        x = x * edge
                    lhs[base + h, a * wanted : (a + 1) * wanted, part * LANES : (part + 1) * LANES] = x.astype(jnp.bfloat16)

    for h in range(2):
        for a in range(leads):
            x = lhs[:, a * wanted : (a + 1) * wanted, :].reshape(RADIX * wanted, width)
            y = jnp.dot(x, inv[:, h * width : (h + 1) * width], preferred_element_type=jnp.float32)
            for g in range(wanted // 8):
                points = []
                for b in range(RADIX):
                    at = b * wanted + g * 8
                    re, im = y[at : at + 8, :LANES], y[at : at + 8, LANES:]
                    c = back[b : b + 1, h * LANES : (h + 1) * LANES]
                    s = back[RADIX + b : RADIX + b + 1, h * LANES : (h + 1) * LANES]
                    if b == 0:
                        points.append((re, None))
                    elif b == RADIX // 2:
                        points.append((re * c - im * s, None))
                    else:
                        points.append((re * c - im * s, re * s + im * c))
                lags = gather8(points)
                for j in range(RADIX):
                    column = (j + RADIX // 2) % RADIX * width + h * LANES
                    out[a * wanted + g * 8 : a * wanted + g * 8 + 8, column : column + LANES] = lags[j]

    send(pl.ds(0, half - 1), x_send, {"section": 1 - sec}, swap).wait_send()
    send(pl.ds(0, half), c_send, {"section": 1 - sec}, swap).wait_send()


def solution(mesh):
    pairs, subs = mesh.shape["pairs"], mesh.shape["sub"]

    def body(raw_record, fir_taps, channel_ids, offsets, pair_table):
        rows, wins = raw_record.shape[0], offsets.shape[0]
        slots = pair_table.shape[0] // pairs
        block = 2 * rows
        leads = block // (2 * subs)
        unit = rows * wins
        assert unit == 8 and block == 8 and wins == 2
        assert rows == HALF
        units = pairs * 2 * subs
        vmem = pl.BlockSpec(memory_space=pltpu.VMEM)
        hbm = pl.BlockSpec(memory_space=pltpu.HBM)
        forward, twiddle, inverse, back = tables()
        total = leads * slots * block
        result = pl.pallas_call(
            functools.partial(kernel, (pairs, subs, rows, wins, slots, leads)),
            out_shape=jax.ShapeDtypeStruct((total, NF), jnp.float32),
            in_specs=[hbm] * 9,
            out_specs=vmem,
            scratch_shapes=[
                pltpu.VMEM((rows, raw_record.shape[1] + LANES), raw_record.dtype),
                pltpu.VMEM((1, TAPS), jnp.float32),
                pltpu.SMEM(channel_ids.shape, jnp.int32),
                pltpu.SMEM(offsets.shape, jnp.int32),
                pltpu.SMEM(pair_table.shape[::-1], jnp.int32),
                pltpu.VMEM(forward.shape, jnp.bfloat16),
                pltpu.VMEM(twiddle.shape, jnp.float32),
                pltpu.SemaphoreType.DMA((7,)),
                pltpu.VMEM((units, 2 * unit, NF // 2), jnp.bfloat16),
                pltpu.VMEM((8, LANES), jnp.float32),
                pltpu.VMEM((2 * LANES, LANES), jnp.float32),
                pltpu.VMEM((4 * leads * subs * unit, 2 * units * unit), jnp.bfloat16),
                pltpu.VMEM((slots * block, 2 * units * unit), jnp.bfloat16),
                pltpu.VMEM((RADIX, total, 2 * LANES), jnp.bfloat16),
                pltpu.VMEM(inverse.shape, jnp.bfloat16),
                pltpu.VMEM(back.shape, jnp.float32),
                pltpu.SemaphoreType.DMA((2,)),
                pltpu.SemaphoreType.DMA,
                pltpu.SemaphoreType.DMA,
                pltpu.SemaphoreType.DMA,
                pltpu.SemaphoreType.DMA((pairs * subs,)),
            ],
            compiler_params=pltpu.CompilerParams(
                collective_id=0, has_side_effects=True, vmem_limit_bytes=48*2**20),
        )(*[pltpu.with_memory_space_constraint(v, pltpu.HBM) for v in (raw_record, fir_taps.reshape(1, TAPS), channel_ids, offsets, pair_table.T,
          jnp.asarray(forward), jnp.asarray(twiddle), jnp.asarray(inverse), jnp.asarray(back))])
        return result.reshape(leads, slots, block, NF)

    return jax.shard_map(
        body,
        mesh=mesh,
        in_specs=(
            P(("groups", "pairs", "section"), "sub"),
            P(),
            P("groups"),
            P(("groups", "sub")),
            P("groups", None),
        ),
        out_specs=P(("section", "sub"), ("groups", "pairs"), None, None),
        check_vma=False,
    )
```
